128 devices in a mesh: frame: 16 (over z_hi, y, core), head: 8 (over z_lo, x).
Axes of the slice: x: 4, y: 4, z: 4 (z_hi: 2, z_lo: 2; z = z_hi * 2 + z_lo), core: 2. Of those that a mesh axis runs over, the one named last changes fastest.
Arguments:
- queries: bfloat16 [32, 512, 3072], P('frame', None, 'head'), may hold values from -24 to 24
- keys: bfloat16 [32, 512, 3072], P('frame', None, 'head'), may hold values from -24 to 24
- values: bfloat16 [32, 512, 3072], P('frame', None, 'head'), may hold values from -6 to 6
- ref_keys: bfloat16 [512, 3072], P('frame', 'head'), may hold values from -24 to 24
- ref_values: bfloat16 [512, 3072], P('frame', 'head'), may hold values from -6 to 6
- rate_scale: float32 [24], P('head'), may hold values from 0.05 to 2
- rate_reach: float32 [24], P('head'), may hold values from 0.1 to 4
- window_start: int32 [32], replicated, may hold values from 0 to 31, as said below
- out_weight: bfloat16 [3072, 3072], P('head'), may hold values from -0.15625 to 0.15625
- conv_taps: float32 [3, 3072], P(None, 'head'), may hold values from -3 to 3
- cotangent: bfloat16 [32, 512, 3072], P('frame', None, 'head'), may hold values from -6 to 6
Outputs:
- block_out: bfloat16 [32, 512, 3072], P('frame', None, 'head')
- grad_queries: bfloat16 [32, 512, 3072], P('frame', None, 'head')
- grad_keys: bfloat16 [32, 512, 3072], P('frame', None, 'head')
- grad_values: bfloat16 [32, 512, 3072], P('frame', None, 'head')
- grad_ref_keys: float32 [512, 3072], P('frame', 'head')
- grad_ref_values: float32 [512, 3072], P('frame', 'head')
- grad_out_weight: float32 [3072, 3072], P('head', 'frame')
- grad_conv_taps: float32 [3, 3072], P(None, 'head')
The draws below stay inside these ranges and needn't reach their ends.
Inputs may be any that keep to these rules, and one draw needn't show every extreme that they name: window_start[f] <= f for every frame f.
All inputs are finite; a program needn't handle non-finite values.
Results may differ from the reference program's by a relative error of at most 0.015.
Values may be sent and summed in bfloat16 or wider, within the bound.
A program may use at most 128 MiB of HBM per device.

```python
import math
import jax
import jax.numpy as jnp
from jax import lax

HEADS = 24
HEAD_DIM = 128
WIDTH = 3072
TAPS = 3
SPATIAL = 512
FRAMES = 32


def draw_queries(key, part):
    noise = jnp.clip(jax.random.normal(jax.random.fold_in(key, 11), (FRAMES, SPATIAL, WIDTH), jnp.float32), -4.0, 4.0)
    return noise.astype(jnp.bfloat16)


def draw_keys(key, part):
    noise = jnp.clip(jax.random.normal(jax.random.fold_in(key, 12), (FRAMES, SPATIAL, WIDTH), jnp.float32), -4.0, 4.0)
    return noise.astype(jnp.bfloat16)


def draw_ref_keys(key, part):
    noise = jnp.clip(jax.random.normal(jax.random.fold_in(key, 13), (SPATIAL, WIDTH), jnp.float32), -4.0, 4.0)
    return noise.astype(jnp.bfloat16)


def draw_window_start(key, part):
    backward_reach = jax.random.randint(jax.random.fold_in(key, 23), (FRAMES,), 0, FRAMES)
    places = jnp.arange(FRAMES, dtype=jnp.int32)
    backward_reach = jnp.where(places == FRAMES - 1, 0, backward_reach)
    return jnp.maximum(places - backward_reach, 0).astype(jnp.int32)


def raised(entries, own_key, source, target, parts, factor):
    def block_of(position):
        return (jnp.arange(entries.shape[position]) // (entries.shape[position] // parts)).reshape((-1,) + (1,) * (entries.ndim - 1 - position))

    first = jax.random.permutation(own_key, parts)[block_of(target)]
    far = (block_of(target) + parts // 2) % parts
    return jnp.where((block_of(source) == first) | (block_of(source) == far), factor * entries, entries)


def steps_of(stream_key, shape, cuts, low, largest):
    def one(position, parts):
        heights = jax.random.uniform(jax.random.fold_in(jax.random.fold_in(stream_key, 6), position), (parts,), jnp.float32, low / len(cuts), largest / len(cuts))
        return jnp.repeat(jnp.exp(heights), shape[position] // parts).reshape((-1,) + (1,) * (len(shape) - position - 1))

    gain = one(*cuts[0])
    for cut in cuts[1:]:
        gain = gain * one(*cut)
    return gain


def bell_draw(rng, extent, spread, most, cuts=(), kind=jnp.bfloat16):
    values = jax.random.normal(rng, extent, jnp.float32) * spread
    if len(cuts) > 0:
        values = steps_of(rng, extent, cuts, -0.22, 0.18) * values
    return jnp.clip(values, min=-most, max=most).astype(kind)


def heavy_noise(own_key, dims, deviation, bound, pieces, heavy, held_as=jnp.bfloat16):
    entries = deviation * jax.random.normal(own_key, dims, jnp.float32)
    if pieces:
        entries = entries * steps_of(own_key, dims, pieces, -0.22, 0.18)
    return jnp.clip(raised(entries, jax.random.fold_in(own_key, 3), *heavy), -bound, bound).astype(held_as)


def setup_inputs(seed: int = 0) -> dict:
    streams_of = jax.random.split(jax.random.key(seed), 12)
    return {
        "queries": draw_queries(jax.random.fold_in(streams_of[11], 71), 0),
        "keys": draw_keys(jax.random.fold_in(streams_of[11], 71), 0),
        "values": bell_draw(streams_of[2], (FRAMES, SPATIAL, WIDTH), 1.0, 6.0, ((0, 16), (2, 8))),
        "ref_keys": draw_ref_keys(jax.random.fold_in(streams_of[11], 71), 0),
        "ref_values": bell_draw(streams_of[4], (SPATIAL, WIDTH), 1.0, 6.0, ((0, 16), (1, 8))),
        "rate_scale": jnp.clip(jnp.exp(math.log(2.0) - 3.6888794 * jax.random.uniform(streams_of[5], (HEADS,), jnp.float32) ** steps_of(streams_of[5], (HEADS,), ((0, 8),), -0.2, 0.2)), 0.05, 2.0),
        "rate_reach": jnp.clip(jnp.exp(math.log(4.0) - 3.6888794 * jax.random.uniform(streams_of[6], (HEADS,), jnp.float32) ** steps_of(streams_of[6], (HEADS,), ((0, 8),), -0.2, 0.2)), 0.1, 4.0),
        "window_start": draw_window_start(jax.random.fold_in(streams_of[11], 71), 0),
        "out_weight": heavy_noise(streams_of[8], (WIDTH, WIDTH), WIDTH ** -0.5, 0.15625, ((0, 8),), (0, 1, 8, 2.0)),
        "conv_taps": bell_draw(streams_of[9], (TAPS, WIDTH), 0.6, 3.0, ((1, 8),), jnp.float32),
        "cotangent": bell_draw(streams_of[10], (FRAMES, SPATIAL, WIDTH), 1.0, 6.0, ((0, 16), (2, 8))),
    }


def kerple_bias(rate_scale, rate_reach, starts):
    count = starts.shape[0]
    places = jnp.arange(count, dtype=jnp.int32)
    distance = jnp.abs(places[:, None] - places[None, :]).astype(jnp.float32)
    penalty = -rate_scale[:, None, None] * jnp.log1p(rate_reach[:, None, None] * distance[None])
    allowed = (places[None, :] <= places[:, None]) & (places[None, :] >= starts[:, None])
    return (penalty, allowed)

def temporal_attend(query_all, key_all, value_all, penalty, allowed):
    frame_count, positions, channels = query_all.shape
    head_count = channels // HEAD_DIM
    query_heads = query_all.reshape(frame_count, positions, head_count, HEAD_DIM)
    key_heads = key_all.reshape(frame_count, positions, head_count, HEAD_DIM)
    value_heads = value_all.reshape(frame_count, positions, head_count, HEAD_DIM)
    scores = jnp.einsum('fphd,gphd->hpfg', query_heads, key_heads) * HEAD_DIM ** (-0.5) + penalty[:, None]
    scores = jnp.where(allowed[None, None], scores, -jnp.inf)
    weights = jax.nn.softmax(scores, axis=-1)
    result = jnp.einsum('hpfg,gphd->fphd', weights, value_heads)
    return result.reshape(frame_count, positions, channels)

def ref_attend(query_all, ref_key_all, ref_value_all):
    frame_count, positions, channels = query_all.shape
    head_count = channels // HEAD_DIM
    key_heads = ref_key_all.reshape(ref_key_all.shape[0], head_count, HEAD_DIM)
    value_heads = ref_value_all.reshape(ref_value_all.shape[0], head_count, HEAD_DIM)

    def one_frame(query_frame):
        query_heads = query_frame.reshape(positions, head_count, HEAD_DIM)
        scores = jnp.einsum('shd,thd->hst', query_heads, key_heads) * HEAD_DIM ** (-0.5)
        weights = jax.nn.softmax(scores, axis=-1)
        return jnp.einsum('hst,thd->shd', weights, value_heads).reshape(positions, channels)
    return lax.map(jax.checkpoint(one_frame), query_all)

def causal_mix(extended, taps, frame_count):
    lead = taps.shape[0] - 1
    result = taps[0] * extended[lead:lead + frame_count]
    for offset in range(1, taps.shape[0]):
        result = result + taps[offset] * extended[lead - offset:lead - offset + frame_count]
    return result

def anti_mix(extended, taps, frame_count):
    result = taps[0] * extended[0:frame_count]
    for offset in range(1, taps.shape[0]):
        result = result + taps[offset] * extended[offset:offset + frame_count]
    return result

def tap_products(grad_out, extended, tap_count):
    lead = tap_count - 1
    frame_count = grad_out.shape[0]
    terms = []
    for offset in range(tap_count):
        terms.append(lax.optimization_barrier(jnp.sum(grad_out * extended[lead - offset:lead - offset + frame_count], axis=(0, 1))))
    return jnp.stack(terms)

def reference(queries, keys, values, ref_keys, ref_values, rate_scale, rate_reach, window_start, out_weight, conv_taps, cotangent):
    penalty, allowed = kerple_bias(rate_scale, rate_reach, window_start)

    def attend(query_all, key_all, value_all, ref_key_all, ref_value_all):
        return temporal_attend(query_all, key_all, value_all, penalty, allowed) + ref_attend(query_all, ref_key_all, ref_value_all)
    summed, pullback = jax.vjp(attend, queries.astype(jnp.float32), keys.astype(jnp.float32), values.astype(jnp.float32), ref_keys.astype(jnp.float32), ref_values.astype(jnp.float32))
    attended = summed.astype(jnp.bfloat16)
    attended_rows = attended.reshape(FRAMES * SPATIAL, WIDTH)
    mixed = jnp.dot(attended_rows, out_weight, preferred_element_type=jnp.float32).astype(jnp.bfloat16)
    lead = TAPS - 1
    past = jnp.concatenate([jnp.zeros((lead, SPATIAL, WIDTH), jnp.float32), mixed.reshape(FRAMES, SPATIAL, WIDTH).astype(jnp.float32)], 0)
    block_out = causal_mix(past, conv_taps, FRAMES).astype(jnp.bfloat16)
    grad_out = cotangent.astype(jnp.float32)
    future = jnp.concatenate([grad_out, jnp.zeros((lead, SPATIAL, WIDTH), jnp.float32)], 0)
    grad_mixed = anti_mix(future, conv_taps, FRAMES).astype(jnp.bfloat16)
    grad_taps = tap_products(grad_out, past, TAPS)
    grad_rows = grad_mixed.reshape(FRAMES * SPATIAL, WIDTH)
    grad_attended = lax.dot_general(grad_rows, out_weight, (((1,), (1,)), ((), ())), preferred_element_type=jnp.float32).astype(jnp.bfloat16)
    grad_weight = lax.dot_general(attended_rows, grad_rows, (((0,), (0,)), ((), ())), preferred_element_type=jnp.float32)
    grads = pullback(grad_attended.reshape(FRAMES, SPATIAL, WIDTH).astype(jnp.float32))
    return (block_out, grads[0].astype(jnp.bfloat16), grads[1].astype(jnp.bfloat16), grads[2].astype(jnp.bfloat16), grads[3], grads[4], grad_weight, grad_taps)
```

```python
import functools

import jax
import jax.numpy as jnp
from jax import lax
from jax.experimental import pallas as pl
from jax.experimental.pallas import tpu as pltpu
from jax.sharding import PartitionSpec as P

HEAD_DIM = 128
HEADS_HERE = 3
FRAMES = 32
GROUPS = 16
PLACES = 32
LANES = 384
REFS = 512
MESH = pl.DeviceIdType.MESH
F32 = jnp.float32
BF16 = jnp.bfloat16
SCALE = HEAD_DIM ** (-0.5)


def dot(a, b):
    return lax.dot_general(a, b, (((1,), (0,)), ((), ())), preferred_element_type=F32)


def dot_nt(a, b):
    return lax.dot_general(a, b, (((1,), (1,)), ((), ())), preferred_element_type=F32)


def dot_tn(a, b):
    return lax.dot_general(a, b, (((0,), (0,)), ((), ())), preferred_element_type=F32)


def softmax_rows(scores):
    top = jnp.max(scores, axis=-1, keepdims=True)
    raised = jnp.exp(scores - top)
    return raised / jnp.sum(raised, axis=-1, keepdims=True)


def kernel(
    q_h, k_h, v_h, c_h, rk_h, rv_h, w_h, taps, bias,
    bo_o, dq_o, dk_o, dv_o, drk_o, drv_o, gwt_o, gt_o,
    pos, ref, w3, wide, att, ab, ga, gb, pr, pt, pm, rh, rb, rz, sz,
    dsend, gws, gwr, drf, drs, drr, bos, gts, gtr,
    loc_sem, in_s, in_r, ag_s, ag_r, rs_s, rs_r, out_s, out_r,
):
    f = lax.axis_index("frame")
    h = lax.axis_index("head")
    plane, x = h // 4, h % 4
    near = plane * 4
    away = (1 - plane) * 4
    xr, xl, xo = (x + 1) % 4, (x + 3) % 4, (x + 2) % 4
    right, left, across = near + xr, near + xl, near + xo
    twin, twin_right, twin_left, twin_across = away + x, away + xr, away + xl, away + xo

    barrier = pltpu.get_barrier_semaphore()

    @pl.loop(1, GROUPS)
    def _(i):
        pl.semaphore_signal(barrier, inc=1, device_id=((f + i) % GROUPS, h), device_id_type=MESH)

    for other in (right, left, twin):
        pl.semaphore_signal(barrier, inc=1, device_id=(f, other), device_id_type=MESH)
    pl.semaphore_wait(barrier, GROUPS + 2)

    def place_in(t, source, i, d, home):
        return pltpu.make_async_remote_copy(
            src_ref=source.at[:, pl.ds(d * PLACES, PLACES), :],
            dst_ref=pos.at[t, pl.ds(home * 2, 2)],
            send_sem=in_s.at[t, i],
            recv_sem=in_r.at[t, i],
            device_id=(d, h),
            device_id_type=MESH,
        )

    def ref_in(t, source, i, d, home):
        return pltpu.make_async_remote_copy(
            src_ref=source,
            dst_ref=ref.at[t, pl.ds(home * PLACES, PLACES), :],
            send_sem=in_s.at[4 + t, i],
            recv_sem=in_r.at[4 + t, i],
            device_id=(d, h),
            device_id_type=MESH,
        )

    def rows_out(t, buffer, out, i, d, home):
        return pltpu.make_async_remote_copy(
            src_ref=buffer.at[pl.ds(d * 2, 2)],
            dst_ref=out.at[:, pl.ds(home * PLACES, PLACES), :],
            send_sem=out_s.at[t, i],
            recv_sem=out_r.at[t, i],
            device_id=(d, h),
            device_id_type=MESH,
        )

    def weight_out(i, d, home):
        return pltpu.make_async_remote_copy(
            src_ref=gws.at[d], dst_ref=gwr.at[home], send_sem=out_s.at[4, i], recv_sem=out_r.at[4, i],
            device_id=(d, h), device_id_type=MESH,
        )

    def refs_out(i, d, home):
        return pltpu.make_async_remote_copy(
            src_ref=drs.at[:, pl.ds(d * PLACES, PLACES), :], dst_ref=drr.at[home],
            send_sem=out_s.at[5, i], recv_sem=out_r.at[5, i],
            device_id=(d, h), device_id_type=MESH,
        )

    def taps_out(i, d, home):
        return pltpu.make_async_remote_copy(
            src_ref=gts, dst_ref=gtr.at[home], send_sem=out_s.at[6, i], recv_sem=out_r.at[6, i],
            device_id=(d, h), device_id_type=MESH,
        )

    def start_all(*makers):
        @pl.loop(1, GROUPS)
        def _(i):
            for maker in makers:
                maker(i, (f + i) % GROUPS, f).start()

    def recv_all(*makers):
        @pl.loop(1, GROUPS)
        def _(i):
            for maker in makers:
                maker(i, f, (f + GROUPS - i) % GROUPS).wait_recv()

    def sent_all(*makers):
        @pl.loop(1, GROUPS)
        def _(i):
            for maker in makers:
                maker(i, (f + i) % GROUPS, f).wait_send()

    ins = [functools.partial(place_in, t, s) for t, s in enumerate((c_h, q_h, k_h, v_h))]
    ref_ins = [functools.partial(ref_in, t, s) for t, s in enumerate((rk_h, rv_h))]
    own_in = [
        pltpu.make_async_copy(s.at[:, pl.ds(f * PLACES, PLACES), :], pos.at[t, pl.ds(f * 2, 2)], loc_sem.at[t])
        for t, s in enumerate((c_h, q_h, k_h, v_h))
    ]
    own_ref = [
        pltpu.make_async_copy(s, ref.at[t, pl.ds(f * PLACES, PLACES), :], loc_sem.at[4 + t])
        for t, s in enumerate((rk_h, rv_h))
    ]
    w_in = [
        pltpu.make_async_copy(w_h.at[:, pl.ds(n * LANES, LANES)], w3.at[n], loc_sem.at[6 + n]) for n in range(8)
    ]
    own_in[0].start()
    start_all(ins[0])
    start_all(*ref_ins)
    start_all(ins[1])
    start_all(ins[2])
    start_all(ins[3])
    for copy in own_in[1:] + own_ref + w_in:
        copy.start()

    own_in[0].wait()
    recv_all(ins[0])
    tap = [taps[n : n + 1, :] for n in range(3)]

    def ct(n):
        return pos[0, n].astype(F32)

    @pl.loop(0, FRAMES - 2)
    def _(n):
        wide[h, n] = (tap[0] * ct(n) + tap[1] * ct(n + 1) + tap[2] * ct(n + 2)).astype(BF16)

    wide[h, FRAMES - 2] = (tap[0] * ct(FRAMES - 2) + tap[1] * ct(FRAMES - 1)).astype(BF16)
    wide[h, FRAMES - 1] = (tap[0] * ct(FRAMES - 1)).astype(BF16)

    def gather(n, slot, low, count, device):
        part = wide.at[slot, pl.ds(low, count)]
        return pltpu.make_async_remote_copy(
            src_ref=part, dst_ref=part, send_sem=ag_s.at[n], recv_sem=ag_r.at[n],
            device_id=(f, device), device_id_type=MESH,
        )

    half = FRAMES // 2
    sends = [
        gather(0, h, 0, FRAMES, right),
        gather(1, h, 0, FRAMES, left),
        gather(2, h, 0, FRAMES, twin),
        gather(3, left, 0, half, right),
        gather(4, right, half, half, left),
        gather(5, twin, 0, FRAMES, right),
        gather(6, twin, 0, FRAMES, left),
        gather(7, twin_left, 0, half, right),
        gather(8, twin_right, half, half, left),
    ]
    arrivals = [
        gather(0, left, 0, FRAMES, right),
        gather(1, right, 0, FRAMES, left),
        gather(2, twin, 0, FRAMES, twin),
        gather(3, across, 0, half, right),
        gather(4, across, half, half, left),
        gather(5, twin_left, 0, FRAMES, right),
        gather(6, twin_right, 0, FRAMES, left),
        gather(7, twin_across, 0, half, right),
        gather(8, twin_across, half, half, left),
    ]
    for n in range(3):
        sends[n].start()

    own_in[1].wait()
    for copy in own_ref:
        copy.wait()
    recv_all(*ref_ins)
    recv_all(ins[1])

    def head_lanes(a):
        return pl.ds(pl.multiple_of(a * HEAD_DIM, HEAD_DIM), HEAD_DIM)

    @pl.loop(0, 12)
    def _(n):
        lanes = head_lanes(n // 4)
        frames = pl.ds((n % 4) * 8, 8)
        query = pos[1, frames, :, lanes].reshape(256, HEAD_DIM)
        weights = softmax_rows(dot_nt(query, ref[0, :, lanes]) * SCALE).astype(BF16)
        pr[n] = weights
        att[frames, :, lanes] = dot(weights, ref[1, :, lanes]).reshape(8, PLACES, HEAD_DIM)

    arrivals[0].wait_recv()
    sends[3].start()
    arrivals[1].wait_recv()
    sends[4].start()

    for t in (2, 3):
        own_in[t].wait()
        recv_all(ins[t])

    def halves(block):
        block = block.astype(F32)
        return [block[:, 8 * n : 8 * n + 8, :].reshape(256, HEAD_DIM).astype(BF16) for n in range(2)]

    def joined(parts):
        return jnp.concatenate([p.reshape(FRAMES, 8, HEAD_DIM) for p in parts], axis=1)

    @pl.loop(0, 6)
    def _(n):
        a, b = n // 2, n % 2
        lanes = head_lanes(a)
        places = pl.ds(pl.multiple_of(b * 16, 16), 16)
        queries = halves(pos[1, :, places, lanes])
        keys = halves(pos[2, :, places, lanes])
        values = halves(pos[3, :, places, lanes])
        parts = []
        for m in range(2):
            weights = softmax_rows(dot_nt(queries[m], keys[m]) * SCALE + bias[a]).astype(BF16)
            pt[n * 2 + m] = weights
            parts.append(dot(weights, values[m]))
        ab[:, places, lanes] = (att[:, places, lanes] + joined(parts)).astype(BF16)

    arrivals[2].wait_recv()
    sends[5].start()
    sends[6].start()

    for copy in w_in:
        copy.wait()

    def rows(array, n):
        return array[pl.ds(n * 8, 8)].reshape(256, LANES)

    @pl.loop(0, 32)
    def _(n):
        slot, part = n // 4, n % 4
        terms = dot(rows(ab, part), w3[slot])
        pm[slot, pl.ds(part * 8, 8)] = terms.astype(BF16).reshape(8, PLACES, LANES)

    def scatter(n, buffer_from, low, slot_buffer, device):
        return pltpu.make_async_remote_copy(
            src_ref=buffer_from.at[pl.ds(low, half)], dst_ref=slot_buffer, send_sem=rs_s.at[n], recv_sem=rs_r.at[n],
            device_id=(f, device), device_id_type=MESH,
        )

    def rounds(o, to_right, to_left, to_across):
        return [
            scatter(o * 6 + 0, pm.at[to_across], 0, rh.at[0, o], right),
            scatter(o * 6 + 1, pm.at[to_across], half, rh.at[1, o], left),
            scatter(o * 6 + 2, pm.at[to_right], half, rb.at[0, o, pl.ds(half, half)], right),
            scatter(o * 6 + 3, pm.at[to_left], 0, rb.at[1, o, pl.ds(0, half)], left),
            scatter(o * 6 + 4, pm.at[to_right], 0, rb.at[0, o, pl.ds(0, half)], right),
            scatter(o * 6 + 5, pm.at[to_left], half, rb.at[1, o, pl.ds(half, half)], left),
        ]

    far = rounds(0, twin_right, twin_left, twin_across)
    own = rounds(1, right, left, across)

    def add_terms(slot, first=False):
        @pl.loop(0, 4)
        def _(n):
            frames = pl.ds(n * 8, 8)
            terms = dot_nt(rows(wide.at[slot], n), w3[slot]).reshape(8, PLACES, LANES)
            ga[frames] = terms if first else ga[frames] + terms

    add_terms(h, True)
    add_terms(left)
    add_terms(right)
    add_terms(twin)
    arrivals[5].wait_recv()
    sends[7].start()
    arrivals[6].wait_recv()
    sends[8].start()
    for n in (0, 1):
        far[n].start()
        own[n].start()
    for n in (2, 3):
        far[n].start()
        own[n].start()
    arrivals[3].wait_recv()
    arrivals[4].wait_recv()
    add_terms(across)
    add_terms(twin_left)
    add_terms(twin_right)

    def weight_terms(slot):
        def body(n, total):
            return total + dot_tn(rows(wide.at[slot], n), rows(ab, n))

        total = lax.fori_loop(0, 4, body, jnp.zeros((LANES, LANES), F32)).astype(BF16)
        gws[slot * 2] = total[:192]
        gws[slot * 2 + 1] = total[192:]

    for slot in (h, left, right, twin, across, twin_left, twin_right):
        weight_terms(slot)
    arrivals[7].wait_recv()
    arrivals[8].wait_recv()
    weight_terms(twin_across)
    start_all(weight_out)
    add_terms(twin_across)

    @pl.loop(0, 4)
    def _(n):
        frames = pl.ds(n * 8, 8)
        gb[frames] = ga[frames].astype(BF16)

    def combine(stage, o, to_right, to_left):
        def add(slot, low, got):
            @pl.loop(0, 4)
            def _(n):
                frames = pl.ds(low + n * 4, 4)
                total = pm[slot, frames].astype(F32) + rh[got, o, pl.ds(n * 4, 4)].astype(F32)
                pm[slot, frames] = total.astype(BF16)

        stage[0].wait_recv()
        add(to_right, 0, 0)
        stage[4].start()
        stage[1].wait_recv()
        add(to_left, half, 1)
        stage[5].start()

    def ref_back(a):
        lanes = pl.ds(a * HEAD_DIM, HEAD_DIM)
        drf[:, :, lanes] = jnp.zeros((2, REFS, HEAD_DIM), F32)

        @pl.loop(0, 4)
        def _(n):
            frames = pl.ds(n * 8, 8)
            grad = gb[frames, :, lanes].reshape(256, HEAD_DIM)
            query = pos[1, frames, :, lanes].reshape(256, HEAD_DIM)
            weights = pr[a * 4 + n]
            slopes = dot_nt(grad, ref[1, :, lanes])
            wide_weights = weights.astype(F32)
            level = jnp.sum(wide_weights * slopes, axis=-1, keepdims=True)
            turned = (wide_weights * (slopes - level) * SCALE).astype(BF16)
            att[frames, :, lanes] = dot(turned, ref[0, :, lanes]).reshape(8, PLACES, HEAD_DIM)
            drf[0, :, lanes] += dot_tn(turned, query)
            drf[1, :, lanes] += dot_tn(weights, grad)

    ref_back(0)
    combine(far, 0, twin_right, twin_left)
    ref_back(1)
    combine(own, 1, right, left)
    ref_back(2)
    for t in range(2):
        drs[t] = drf[t].astype(BF16)
    start_all(refs_out)

    @pl.loop(0, 6)
    def _(n):
        a, b = n // 2, n % 2
        lanes = head_lanes(a)
        places = pl.ds(pl.multiple_of(b * 16, 16), 16)
        queries = halves(pos[1, :, places, lanes])
        keys = halves(pos[2, :, places, lanes])
        values = halves(pos[3, :, places, lanes])
        grads = halves(gb[:, places, lanes])
        parts = [[], [], []]
        for m in range(2):
            weights = pt[n * 2 + m]
            slopes = dot_nt(grads[m], values[m])
            wide_weights = weights.astype(F32)
            level = jnp.sum(wide_weights * slopes, axis=-1, keepdims=True)
            turned = (wide_weights * (slopes - level) * SCALE).astype(BF16)
            parts[0].append(dot(turned, keys[m]))
            parts[1].append(dot_tn(turned, queries[m]))
            parts[2].append(dot_tn(weights, grads[m]))
        dsend[0, :, places, lanes] = (att[:, places, lanes] + joined(parts[0])).astype(BF16)
        dsend[1, :, places, lanes] = joined(parts[1]).astype(BF16)
        dsend[2, :, places, lanes] = joined(parts[2]).astype(BF16)

    grads_out = [functools.partial(rows_out, t, dsend.at[t], o) for t, o in enumerate((dq_o, dk_o, dv_o))]
    own_out = [
        pltpu.make_async_copy(dsend.at[t, pl.ds(f * 2, 2)], o.at[:, pl.ds(f * PLACES, PLACES), :], loc_sem.at[14 + t])
        for t, o in enumerate((dq_o, dk_o, dv_o))
    ]
    for t in range(3):
        start_all(grads_out[t])
        own_out[t].start()

    for n in (2, 3, 4, 5):
        far[n].wait_recv()

    @pl.loop(0, 8)
    def _(n):
        frames = pl.ds(n * 4, 4)
        total = pm[twin, frames].astype(F32) + rb[0, 0, frames].astype(F32) + rb[1, 0, frames].astype(F32)
        sz[frames] = total.astype(BF16)

    twin_sum = pltpu.make_async_remote_copy(
        src_ref=sz, dst_ref=rz, send_sem=rs_s.at[12], recv_sem=rs_r.at[12], device_id=(f, twin), device_id_type=MESH
    )
    twin_sum.start()
    for n in (2, 3, 4, 5):
        own[n].wait_recv()

    @pl.loop(0, 8)
    def _(n):
        frames = pl.ds(n * 4, 4)
        ga[frames] = pm[h, frames].astype(F32) + rb[0, 1, frames].astype(F32) + rb[1, 1, frames].astype(F32)

    twin_sum.wait_recv()

    @pl.loop(0, 8)
    def _(n):
        frames = pl.ds(n * 4, 4)
        ga[frames] = (ga[frames] + rz[frames].astype(F32)).astype(BF16).astype(F32)

    gts[...] = jnp.zeros_like(gts)
    bos[0] = (tap[0] * ga[0]).astype(BF16)
    bos[1] = (tap[0] * ga[1] + tap[1] * ga[0]).astype(BF16)
    c0, c1 = ct(0), ct(1)
    sums = (c0 * ga[0] + c1 * ga[1], c1 * ga[0], jnp.zeros((PLACES, LANES), F32))

    def mix(n, carry):
        now, back, older = ga[n], ga[n - 1], ga[n - 2]
        bos[n] = (tap[0] * now + tap[1] * back + tap[2] * older).astype(BF16)
        c = ct(n)
        return (carry[0] + c * now, carry[1] + c * back, carry[2] + c * older)

    sums = lax.fori_loop(2, FRAMES, mix, sums)
    block_out = functools.partial(rows_out, 3, bos, bo_o)
    start_all(block_out)
    own_block = pltpu.make_async_copy(bos.at[pl.ds(f * 2, 2)], bo_o.at[:, pl.ds(f * PLACES, PLACES), :], loc_sem.at[17])
    own_block.start()
    for n in range(3):
        gts[n : n + 1, :] = jnp.sum(sums[n], axis=0, keepdims=True)
    start_all(taps_out)

    recv_all(weight_out)

    def weight_sum(i, total):
        return total + gwr[(f + i) % GROUPS].astype(F32)

    gwt_o[...] = lax.fori_loop(1, GROUPS, weight_sum, gws[f].astype(F32))
    recv_all(refs_out)

    def refs_sum(i, total):
        return total + drr[(f + i) % GROUPS].astype(F32)

    mine = drs[:, pl.ds(f * PLACES, PLACES), :].astype(F32)
    both = lax.fori_loop(1, GROUPS, refs_sum, mine)
    drk_o[...] = both[0]
    drv_o[...] = both[1]
    recv_all(taps_out)
    gt_o[...] = lax.fori_loop(1, GROUPS, lambda i, total: total + gtr[(f + i) % GROUPS], gts[...])

    recv_all(*grads_out)
    recv_all(block_out)
    for copy in own_out:
        copy.wait()
    own_block.wait()
    sent_all(*ins, *ref_ins, weight_out, refs_out, taps_out, *grads_out, block_out)
    for copy in sends + far + own + [twin_sum]:
        copy.wait_send()


def per_device(queries, keys, values, ref_keys, ref_values, rate_scale, rate_reach, starts, weight, taps, cotangent):
    places = jnp.arange(256, dtype=jnp.int32)
    frame, place = places // 8, places % 8
    distance = jnp.abs(frame[:, None] - frame[None, :]).astype(F32)
    first = jnp.repeat(starts, 8)
    allowed = (
        (place[:, None] == place[None, :])
        & (frame[None, :] <= frame[:, None])
        & (frame[None, :] >= first[:, None])
    )
    penalty = -rate_scale[:, None, None] * jnp.log1p(rate_reach[:, None, None] * distance[None])
    bias = jnp.where(allowed[None], penalty, -1e30)

    anywhere = pl.BlockSpec(memory_space=pl.ANY)
    vmem = pl.BlockSpec(memory_space=pltpu.VMEM)
    rows = (FRAMES, PLACES, LANES)
    video = jax.ShapeDtypeStruct(queries.shape, BF16)
    refs = jax.ShapeDtypeStruct(ref_keys.shape, F32)
    outs = pl.pallas_call(
        kernel,
        out_shape=[
            video, video, video, video, refs, refs,
            jax.ShapeDtypeStruct((192, LANES), F32),
            jax.ShapeDtypeStruct((8, LANES), F32),
        ],
        in_specs=[anywhere] * 7 + [vmem] * 2,
        out_specs=[anywhere] * 4 + [vmem] * 4,
        scratch_shapes=[
            pltpu.VMEM((4,) + rows, BF16),
            pltpu.VMEM((2, REFS, LANES), BF16),
            pltpu.VMEM((8, LANES, LANES), BF16),
            pltpu.VMEM((8,) + rows, BF16),
            pltpu.VMEM(rows, F32),
            pltpu.VMEM(rows, BF16),
            pltpu.VMEM(rows, F32),
            pltpu.VMEM(rows, BF16),
            pltpu.VMEM((12, 256, REFS), BF16),
            pltpu.VMEM((12, 256, 256), BF16),
            pltpu.VMEM((8,) + rows, BF16),
            pltpu.VMEM((2, 2, 16, PLACES, LANES), BF16),
            pltpu.VMEM((2, 2) + rows, BF16),
            pltpu.VMEM(rows, BF16),
            pltpu.VMEM(rows, BF16),
            pltpu.VMEM((3,) + rows, BF16),
            pltpu.VMEM((GROUPS, 192, LANES), BF16),
            pltpu.VMEM((GROUPS, 192, LANES), BF16),
            pltpu.VMEM((2, REFS, LANES), F32),
            pltpu.VMEM((2, REFS, LANES), BF16),
            pltpu.VMEM((GROUPS, 2, PLACES, LANES), BF16),
            pltpu.VMEM(rows, BF16),
            pltpu.VMEM((8, LANES), F32),
            pltpu.VMEM((GROUPS, 8, LANES), F32),
            pltpu.SemaphoreType.DMA((18,)),
            pltpu.SemaphoreType.DMA((6, GROUPS)),
            pltpu.SemaphoreType.DMA((6, GROUPS)),
            pltpu.SemaphoreType.DMA((9,)),
            pltpu.SemaphoreType.DMA((9,)),
            pltpu.SemaphoreType.DMA((13,)),
            pltpu.SemaphoreType.DMA((13,)),
            pltpu.SemaphoreType.DMA((7, GROUPS)),
            pltpu.SemaphoreType.DMA((7, GROUPS)),
        ],
        compiler_params=pltpu.CompilerParams(
            collective_id=0, has_side_effects=True, vmem_limit_bytes=64_000_000
        ),
    )(queries, keys, values, cotangent, ref_keys, ref_values, weight, taps, bias)
    block_out, grad_q, grad_k, grad_v, grad_rk, grad_rv, grad_w, grad_taps = outs
    return block_out, grad_q, grad_k, grad_v, grad_rk, grad_rv, grad_w.T, grad_taps[:3]


def solution(mesh):
    video = P("frame", None, "head")
    return jax.shard_map(
        per_device,
        mesh=mesh,
        in_specs=(
            video, video, video, P("frame", "head"), P("frame", "head"),
            P("head"), P("head"), P(), P("head", None), P(None, "head"), video,
        ),
        out_specs=(
            video, video, video, video, P("frame", "head"), P("frame", "head"), P("head", "frame"), P(None, "head"),
        ),
        check_vma=False,
    )
```

```python
import functools

import jax
import jax.numpy as jnp
from jax import lax
from jax.experimental import pallas as pl
from jax.experimental.pallas import tpu as pltpu
from jax.sharding import PartitionSpec as P

HEAD_DIM = 128
HEADS_HERE = 3
FRAMES = 32
GROUPS = 16
PLACES = 32
LANES = 384
REFS = 512
MESH = pl.DeviceIdType.MESH
F32 = jnp.float32
BF16 = jnp.bfloat16
SCALE = HEAD_DIM ** (-0.5)


def dot(a, b):
    return lax.dot_general(a, b, (((1,), (0,)), ((), ())), preferred_element_type=F32)


def dot_nt(a, b):
    return lax.dot_general(a, b, (((1,), (1,)), ((), ())), preferred_element_type=F32)


def dot_tn(a, b):
    return lax.dot_general(a, b, (((0,), (0,)), ((), ())), preferred_element_type=F32)


def softmax_rows(scores):
    top = jnp.max(scores, axis=-1, keepdims=True)
    raised = jnp.exp(scores - top)
    return raised / jnp.sum(raised, axis=-1, keepdims=True)


def kernel(
    q_h, k_h, v_h, c_h, rk_h, rv_h, w_h, taps, bias,
    bo_o, dq_o, dk_o, dv_o, drk_o, drv_o, gwt_o, gt_o,
    pos, ref, w3, wide, att, ab, ga, gb, pr, pt, pm, rh, rb, rz, sz,
    dsend, gws, g1, g2, g3, g4, grs, r1, r2, r3, r4, drf, bos, gts, gtr,
    loc_sem, hop_s, hop_r, in_s, in_r, ag_s, ag_r, rs_s, rs_r, out_s, out_r,
):
    f = lax.axis_index("frame")
    h = lax.axis_index("head")
    plane, x = h // 4, h % 4
    near = plane * 4
    away = (1 - plane) * 4
    xr, xl, xo = (x + 1) % 4, (x + 3) % 4, (x + 2) % 4
    right, left, across = near + xr, near + xl, near + xo
    twin, twin_right, twin_left, twin_across = away + x, away + xr, away + xl, away + xo
    zh, y, c = f // 8, (f // 2) % 4, f % 2
    half = FRAMES // 2
    later, sooner = pl.ds(half, half), pl.ds(0, half)
    sides = [pl.ds(0, 16), pl.ds(16, 16)]

    barrier = pltpu.get_barrier_semaphore()

    @pl.loop(1, GROUPS)
    def _(i):
        pl.semaphore_signal(barrier, inc=1, device_id=((f + i) % GROUPS, h), device_id_type=MESH)

    for other in (right, left, twin):
        pl.semaphore_signal(barrier, inc=1, device_id=(f, other), device_id_type=MESH)
    pl.semaphore_wait(barrier, GROUPS + 2)

    def place_in(t, source, i, d, home):
        return pltpu.make_async_remote_copy(
            src_ref=source.at[:, pl.ds(d * PLACES, PLACES), :],
            dst_ref=pos.at[t, pl.ds(home * 2, 2)],
            send_sem=in_s.at[t, i],
            recv_sem=in_r.at[t, i],
            device_id=(d, h),
            device_id_type=MESH,
        )

    def rows_out(t, b, buffer, out, i, d, home):
        return pltpu.make_async_remote_copy(
            src_ref=buffer.at[pl.ds(d * 2, 2), sides[b]],
            dst_ref=out.at[:, pl.ds(home * PLACES + b * 16, 16), :],
            send_sem=out_s.at[t * 2 + b, i],
            recv_sem=out_r.at[t * 2 + b, i],
            device_id=(d, h),
            device_id_type=MESH,
        )

    def own_rows(t, b, buffer, out):
        return pltpu.make_async_copy(
            buffer.at[pl.ds(f * 2, 2), sides[b]],
            out.at[:, pl.ds(f * PLACES + b * 16, 16), :],
            loc_sem.at[14 + t * 2 + b],
        )

    def device(zh_to, y_to, c_to):
        return ((zh_to * 4 + y_to) * 2 + c_to, h)

    z_mate, c_mate = device(1 - zh, y, c), device(zh, y, 1 - c)

    def hop(n, source, target, to):
        return pltpu.make_async_remote_copy(
            src_ref=source, dst_ref=target, send_sem=hop_s.at[n], recv_sem=hop_r.at[n],
            device_id=to, device_id_type=MESH,
        )

    ref_z = [hop(t, s, ref.at[t, zh, y, c], z_mate) for t, s in enumerate((rk_h, rv_h))]
    ref_z_here = [hop(t, s, ref.at[t, 1 - zh, y, c], z_mate) for t, s in enumerate((rk_h, rv_h))]

    def ref_y(n, y_from):
        part = ref.at[:, :, y_from, c]
        return hop(1 + n, part, part, device(zh, (y + n) % 4, c))

    def ref_c(c_from):
        part = ref.at[:, :, :, c_from]
        return hop(5, part, part, c_mate)

    class Sum:
        def __init__(self, base, src, b1, b2, b3, b4):
            self.base, self.src, self.b1, self.b2, self.b3, self.b4 = base, src, b1, b2, b3, b4
            self.to_core = hop(base, src.at[1 - c], b1, c_mate)
            self.to_z = hop(base + 4, b3.at[1 - zh], b4, z_mate)

        def to_y(self, n, y_of):
            return hop(self.base + n, self.src.at[c, y_of], self.b2.at[n - 1], device(zh, (y + n) % 4, c))

        def cores_done(self):
            self.to_core.wait_recv()
            for n in range(4):
                for m in range(2):
                    total = self.src[c, n, m].astype(F32) + self.b1[n, m].astype(F32)
                    self.src[c, n, m] = total.astype(BF16)
            for n in (1, 2, 3):
                self.to_y(n, (y + n) % 4).start()

        def rows_done(self):
            for n in (1, 2, 3):
                self.to_y(n, y).wait_recv()
            for m in range(2):
                total = self.src[c, y, m].astype(F32)
                for n in range(3):
                    total = total + self.b2[n, m].astype(F32)
                self.b3[m] = total.astype(BF16)
            self.to_z.start()

        def total(self):
            self.to_z.wait_recv()
            return self.b3[zh].astype(F32) + self.b4[...].astype(F32)

        def started(self):
            return [self.to_core, self.to_z] + [self.to_y(n, (y + n) % 4) for n in (1, 2, 3)]

    weight_grad = Sum(6, gws, g1, g2, g3, g4)
    ref_grad = Sum(11, grs, r1, r2, r3, r4)

    def taps_out(i, d, home):
        return pltpu.make_async_remote_copy(
            src_ref=gts, dst_ref=gtr.at[home], send_sem=out_s.at[8, i], recv_sem=out_r.at[8, i],
            device_id=(d, h), device_id_type=MESH,
        )

    def start_all(*makers):
        @pl.loop(1, GROUPS)
        def _(i):
            for maker in makers:
                maker(i, (f + i) % GROUPS, f).start()

    def recv_all(*makers):
        @pl.loop(1, GROUPS)
        def _(i):
            for maker in makers:
                maker(i, f, (f + GROUPS - i) % GROUPS).wait_recv()

    def sent_all(*makers):
        @pl.loop(1, GROUPS)
        def _(i):
            for maker in makers:
                maker(i, (f + i) % GROUPS, f).wait_send()

    def gather(b, n, slot, frames, to):
        part = wide.at[slot, frames, sides[b]]
        return pltpu.make_async_remote_copy(
            src_ref=part, dst_ref=part, send_sem=ag_s.at[b * 9 + n], recv_sem=ag_r.at[b * 9 + n],
            device_id=(f, to), device_id_type=MESH,
        )

    whole = pl.ds(0, FRAMES)
    sends = [
        [
            gather(b, 0, h, whole, right),
            gather(b, 1, h, whole, left),
            gather(b, 2, h, whole, twin),
            gather(b, 3, left, sooner, right),
            gather(b, 4, right, later, left),
            gather(b, 5, twin, whole, right),
            gather(b, 6, twin, whole, left),
            gather(b, 7, twin_left, sooner, right),
            gather(b, 8, twin_right, later, left),
        ]
        for b in range(2)
    ]
    arrivals = [
        [
            gather(b, 0, left, whole, right),
            gather(b, 1, right, whole, left),
            gather(b, 2, twin, whole, twin),
            gather(b, 3, across, sooner, right),
            gather(b, 4, across, later, left),
            gather(b, 5, twin_left, whole, right),
            gather(b, 6, twin_right, whole, left),
            gather(b, 7, twin_across, sooner, right),
            gather(b, 8, twin_across, later, left),
        ]
        for b in range(2)
    ]

    def send(b, *which):
        for n in which:
            sends[b][n].start()

    def got(b, *which):
        for n in which:
            arrivals[b][n].wait_recv()

    def scatter(b, o, n, slot, frames, target, to):
        at = (b * 2 + o) * 6 + n
        return pltpu.make_async_remote_copy(
            src_ref=pm.at[slot, frames, sides[b]], dst_ref=target, send_sem=rs_s.at[at], recv_sem=rs_r.at[at],
            device_id=(f, to), device_id_type=MESH,
        )

    ways = [(twin_right, twin_left, twin_across), (right, left, across)]

    def rounds(b, o):
        to_right, to_left, to_across = ways[o]
        return [
            scatter(b, o, 0, to_across, sooner, rh.at[0, o, :, sides[b]], right),
            scatter(b, o, 1, to_across, later, rh.at[1, o, :, sides[b]], left),
            scatter(b, o, 2, to_right, later, rb.at[0, o, later, sides[b]], right),
            scatter(b, o, 3, to_left, sooner, rb.at[1, o, sooner, sides[b]], left),
            scatter(b, o, 4, to_right, sooner, rb.at[0, o, sooner, sides[b]], right),
            scatter(b, o, 5, to_left, later, rb.at[1, o, later, sides[b]], left),
        ]

    turns = [[rounds(b, o) for o in range(2)] for b in range(2)]
    twin_sum = [
        pltpu.make_async_remote_copy(
            src_ref=sz.at[:, sides[b]], dst_ref=rz.at[:, sides[b]], send_sem=rs_s.at[24 + b],
            recv_sem=rs_r.at[24 + b], device_id=(f, twin), device_id_type=MESH,
        )
        for b in range(2)
    ]

    ins = [functools.partial(place_in, t, s) for t, s in enumerate((c_h, q_h, k_h, v_h))]
    own_in = [
        pltpu.make_async_copy(s.at[:, pl.ds(f * PLACES, PLACES), :], pos.at[t, pl.ds(f * 2, 2)], loc_sem.at[t])
        for t, s in enumerate((c_h, q_h, k_h, v_h))
    ]
    own_ref = [
        pltpu.make_async_copy(s, ref.at[t, zh, y, c], loc_sem.at[4 + t]) for t, s in enumerate((rk_h, rv_h))
    ]
    w_in = [
        pltpu.make_async_copy(w_h.at[:, pl.ds(n * LANES, LANES)], w3.at[n], loc_sem.at[6 + n]) for n in range(8)
    ]
    for copy in ref_z + own_ref + own_in[:2]:
        copy.start()
    start_all(ins[0])
    start_all(ins[1])
    start_all(ins[2])
    for copy in own_in[2:] + w_in:
        copy.start()
    drf[...] = jnp.zeros_like(drf)
    gts[...] = jnp.zeros_like(gts)

    own_in[0].wait()
    recv_all(ins[0])
    tap = [taps[n : n + 1, :] for n in range(3)]

    def ct(n):
        return pos[0, n].astype(F32)

    @pl.loop(0, FRAMES - 2)
    def _(n):
        wide[h, n] = (tap[0] * ct(n) + tap[1] * ct(n + 1) + tap[2] * ct(n + 2)).astype(BF16)

    wide[h, FRAMES - 2] = (tap[0] * ct(FRAMES - 2) + tap[1] * ct(FRAMES - 1)).astype(BF16)
    wide[h, FRAMES - 1] = (tap[0] * ct(FRAMES - 1)).astype(BF16)
    send(0, 0, 1, 2)
    for copy in own_ref:
        copy.wait()
    for copy in ref_z_here:
        copy.wait_recv()
    for n in (1, 2, 3):
        ref_y(n, y).start()
    got(0, 0, 1)
    send(0, 3, 4)
    send(1, 0, 1)

    for n in (1, 2, 3):
        ref_y(n, (y + 4 - n) % 4).wait_recv()
    ref_c(c).start()
    own_in[1].wait()
    recv_all(ins[1])
    ref_c(1 - c).wait_recv()

    def head_lanes(a):
        return pl.ds(pl.multiple_of(a * HEAD_DIM, HEAD_DIM), HEAD_DIM)

    def ref_rows(t, lanes):
        return ref[t, :, :, :, :, lanes].reshape(REFS, HEAD_DIM)

    def ref_fwd(b):
        @pl.loop(0, 6)
        def _(n):
            lanes = head_lanes(n // 2)
            frames = pl.ds((n % 2) * half, half)
            query = pos[1, frames, sides[b], lanes].reshape(256, HEAD_DIM)
            weights = softmax_rows(dot_nt(query, ref_rows(0, lanes)) * SCALE).astype(BF16)
            pr[b * 6 + n] = weights
            att[frames, sides[b], lanes] = dot(weights, ref_rows(1, lanes)).reshape(half, 16, HEAD_DIM)

    ref_fwd(0)
    got(0, 2)
    send(0, 5, 6)
    send(1, 2)
    start_all(ins[3])
    ref_fwd(1)
    got(1, 0, 1)
    send(1, 3, 4)

    for copy in w_in:
        copy.wait()

    def rows(array, b, n):
        return array[pl.ds(n * half, half), sides[b]].reshape(256, LANES)

    def add_terms(b, slot, first=False):
        for n in range(2):
            frames = pl.ds(n * half, half)
            terms = dot_nt(rows(wide.at[slot], b, n), w3[slot]).reshape(half, 16, LANES)
            ga[frames, sides[b]] = terms if first else ga[frames, sides[b]] + terms

    add_terms(0, h, True)
    add_terms(0, left)
    add_terms(0, right)
    add_terms(0, twin)
    got(0, 5, 6)
    send(0, 7, 8)
    got(0, 3, 4)
    add_terms(0, across)
    add_terms(0, twin_left)
    add_terms(0, twin_right)
    got(1, 2)
    send(1, 5, 6)
    for t in (2, 3):
        own_in[t].wait()
        recv_all(ins[t])

    def halves(block):
        block = block.astype(F32)
        return [block[:, 8 * n : 8 * n + 8, :].reshape(256, HEAD_DIM).astype(BF16) for n in range(2)]

    def joined(parts):
        return jnp.concatenate([p.reshape(FRAMES, 8, HEAD_DIM) for p in parts], axis=1)

    def time_fwd(b):
        @pl.loop(0, 3)
        def _(a):
            lanes = head_lanes(a)
            queries = halves(pos[1, :, sides[b], lanes])
            keys = halves(pos[2, :, sides[b], lanes])
            values = halves(pos[3, :, sides[b], lanes])
            parts = []
            for m in range(2):
                weights = softmax_rows(dot_nt(queries[m], keys[m]) * SCALE + bias[a]).astype(BF16)
                pt[(b * 3 + a) * 2 + m] = weights
                parts.append(dot(weights, values[m]))
            ab[:, sides[b], lanes] = (att[:, sides[b], lanes] + joined(parts)).astype(BF16)

    def project(b):
        @pl.loop(0, 16)
        def _(n):
            slot, part = n // 2, n % 2
            terms = dot(rows(ab, b, part), w3[slot])
            pm[slot, pl.ds(part * half, half), sides[b]] = terms.astype(BF16).reshape(half, 16, LANES)

    def scatter_first(b):
        for o in range(2):
            for n in range(4):
                turns[b][o][n].start()

    def combine(b, o):
        to_right, to_left, _ = ways[o]

        def add(slot, low, side):
            @pl.loop(0, 2)
            def _(n):
                frames = pl.ds(low + n * 8, 8)
                total = pm[slot, frames, sides[b]].astype(F32) + rh[side, o, pl.ds(n * 8, 8), sides[b]].astype(F32)
                pm[slot, frames, sides[b]] = total.astype(BF16)

        turns[b][o][0].wait_recv()
        add(to_right, 0, 0)
        turns[b][o][4].start()
        turns[b][o][1].wait_recv()
        add(to_left, half, 1)
        turns[b][o][5].start()

    def ref_back(b):
        @pl.loop(0, 6)
        def _(n):
            lanes = head_lanes(n // 2)
            frames = pl.ds((n % 2) * half, half)
            grad = gb[frames, sides[b], lanes].reshape(256, HEAD_DIM)
            query = pos[1, frames, sides[b], lanes].reshape(256, HEAD_DIM)
            weights = pr[b * 6 + n]
            slopes = dot_nt(grad, ref_rows(1, lanes))
            wide_weights = weights.astype(F32)
            level = jnp.sum(wide_weights * slopes, axis=-1, keepdims=True)
            turned = (wide_weights * (slopes - level) * SCALE).astype(BF16)
            att[frames, sides[b], lanes] = dot(turned, ref_rows(0, lanes)).reshape(half, 16, HEAD_DIM)
            drf[0, :, lanes] += dot_tn(turned, query)
            drf[1, :, lanes] += dot_tn(weights, grad)

    def time_back(b):
        @pl.loop(0, 3)
        def _(a):
            lanes = head_lanes(a)
            queries = halves(pos[1, :, sides[b], lanes])
            keys = halves(pos[2, :, sides[b], lanes])
            values = halves(pos[3, :, sides[b], lanes])
            grads = halves(gb[:, sides[b], lanes])
            parts = [[], [], []]
            for m in range(2):
                weights = pt[(b * 3 + a) * 2 + m]
                slopes = dot_nt(grads[m], values[m])
                wide_weights = weights.astype(F32)
                level = jnp.sum(wide_weights * slopes, axis=-1, keepdims=True)
                turned = (wide_weights * (slopes - level) * SCALE).astype(BF16)
                parts[0].append(dot(turned, keys[m]))
                parts[1].append(dot_tn(turned, queries[m]))
                parts[2].append(dot_tn(weights, grads[m]))
            dsend[0, :, sides[b], lanes] = (att[:, sides[b], lanes] + joined(parts[0])).astype(BF16)
            dsend[1, :, sides[b], lanes] = joined(parts[1]).astype(BF16)
            dsend[2, :, sides[b], lanes] = joined(parts[2]).astype(BF16)

    grads_out = [
        [functools.partial(rows_out, t, b, dsend.at[t], o) for t, o in enumerate((dq_o, dk_o, dv_o))] for b in range(2)
    ]
    own_grads = [
        [own_rows(t, b, dsend.at[t], o) for t, o in enumerate((dq_o, dk_o, dv_o))] for b in range(2)
    ]

    def grads_away(b):
        for t in range(3):
            start_all(grads_out[b][t])
        for copy in own_grads[b]:
            copy.start()

    def round_grad(b):
        @pl.loop(0, 4)
        def _(n):
            frames = pl.ds(n * 8, 8)
            gb[frames, sides[b]] = ga[frames, sides[b]].astype(BF16)

    time_fwd(0)
    time_fwd(1)
    project(0)
    scatter_first(0)
    got(0, 7, 8)
    add_terms(0, twin_across)
    round_grad(0)
    ref_back(0)
    got(1, 5, 6)
    send(1, 7, 8)
    time_back(0)
    grads_away(0)
    def plane_sum(b):
        for n in (2, 3, 4, 5):
            turns[b][0][n].wait_recv()

        @pl.loop(0, 4)
        def _(n):
            frames = pl.ds(n * 8, 8)
            total = pm[twin, frames, sides[b]].astype(F32)
            for side in range(2):
                total = total + rb[side, 0, frames, sides[b]].astype(F32)
            sz[frames, sides[b]] = total.astype(BF16)

        twin_sum[b].start()

    combine(0, 0)
    combine(0, 1)
    project(1)
    scatter_first(1)
    add_terms(1, h, True)
    for slot in (left, right, twin):
        add_terms(1, slot)
    got(1, 3, 4)
    for slot in (across, twin_left, twin_right):
        add_terms(1, slot)
    got(1, 7, 8)
    plane_sum(0)

    @pl.loop(0, 8)
    def _(slot):
        total = dot_tn(wide[slot].reshape(1024, LANES), ab[...].reshape(1024, LANES)).astype(BF16)
        for j in range(2):
            gws[j, slot % 4, slot // 4] = total[192 * j : 192 * j + 192]

    weight_grad.to_core.start()
    add_terms(1, twin_across)
    round_grad(1)
    ref_back(1)
    weight_grad.cores_done()
    combine(1, 0)
    time_back(1)
    grads_away(1)
    combine(1, 1)
    for d in range(GROUPS):
        for t in range(2):
            part = drf[t, d * PLACES : (d + 1) * PLACES].astype(BF16)
            grs[d % 2, (d // 2) % 4, d // 8, t * PLACES : (t + 1) * PLACES] = part
    ref_grad.to_core.start()
    plane_sum(1)
    ref_grad.cores_done()

    def plane_own(b):
        for n in (2, 3, 4, 5):
            turns[b][1][n].wait_recv()

    def output(b):
        @pl.loop(0, 4)
        def _(n):
            frames = pl.ds(n * 8, 8)
            total = pm[h, frames, sides[b]].astype(F32) + rz[frames, sides[b]].astype(F32)
            for side in range(2):
                total = total + rb[side, 1, frames, sides[b]].astype(F32)
            ga[frames, sides[b]] = total.astype(BF16).astype(F32)

        def cs(n):
            return pos[0, n, sides[b]].astype(F32)

        def mixed(n):
            return ga[n, sides[b]]

        bos[0, sides[b]] = (tap[0] * mixed(0)).astype(BF16)
        bos[1, sides[b]] = (tap[0] * mixed(1) + tap[1] * mixed(0)).astype(BF16)
        sums = (cs(0) * mixed(0) + cs(1) * mixed(1), cs(1) * mixed(0), jnp.zeros((16, LANES), F32))

        def mix(n, carry):
            now, back, older = mixed(n), mixed(n - 1), mixed(n - 2)
            bos[n, sides[b]] = (tap[0] * now + tap[1] * back + tap[2] * older).astype(BF16)
            cn = cs(n)
            return (carry[0] + cn * now, carry[1] + cn * back, carry[2] + cn * older)

        sums = lax.fori_loop(2, FRAMES, mix, sums)
        start_all(block_out[b])
        own_block[b].start()
        for n in range(3):
            gts[n : n + 1, :] += jnp.sum(sums[n], axis=0, keepdims=True)

    block_out = [functools.partial(rows_out, 3, b, bos, bo_o) for b in range(2)]
    own_block = [own_rows(3, b, bos, bo_o) for b in range(2)]
    plane_own(0)
    twin_sum[0].wait_recv()
    output(0)
    plane_own(1)
    weight_grad.rows_done()
    ref_grad.rows_done()
    twin_sum[1].wait_recv()
    output(1)
    start_all(taps_out)
    gwt_o[...] = weight_grad.total()
    refs = ref_grad.total()
    drk_o[...] = refs[:PLACES]
    drv_o[...] = refs[PLACES:]

    recv_all(taps_out)
    gt_o[...] = lax.fori_loop(1, GROUPS, lambda i, total: total + gtr[(f + i) % GROUPS], gts[...])
    recv_all(*grads_out[0], *grads_out[1])
    recv_all(*block_out)
    for copy in own_grads[0] + own_grads[1] + own_block:
        copy.wait()
    sent_all(*ins, taps_out, *grads_out[0], *grads_out[1], *block_out)
    steps = ref_z + [ref_y(n, y) for n in (1, 2, 3)] + [ref_c(c)]
    steps += weight_grad.started() + ref_grad.started()
    for b in range(2):
        steps += sends[b] + turns[b][0] + turns[b][1] + [twin_sum[b]]
    for copy in steps:
        copy.wait_send()


def per_device(queries, keys, values, ref_keys, ref_values, rate_scale, rate_reach, starts, weight, taps, cotangent):
    places = jnp.arange(256, dtype=jnp.int32)
    frame, place = places // 8, places % 8
    distance = jnp.abs(frame[:, None] - frame[None, :]).astype(F32)
    first = jnp.repeat(starts, 8)
    allowed = (
        (place[:, None] == place[None, :])
        & (frame[None, :] <= frame[:, None])
        & (frame[None, :] >= first[:, None])
    )
    penalty = -rate_scale[:, None, None] * jnp.log1p(rate_reach[:, None, None] * distance[None])
    bias = jnp.where(allowed[None], penalty, -1e30)

    anywhere = pl.BlockSpec(memory_space=pl.ANY)
    vmem = pl.BlockSpec(memory_space=pltpu.VMEM)
    rows = (FRAMES, PLACES, LANES)
    video = jax.ShapeDtypeStruct(queries.shape, BF16)
    refs = jax.ShapeDtypeStruct(ref_keys.shape, F32)
    outs = pl.pallas_call(
        kernel,
        out_shape=[
            video, video, video, video, refs, refs,
            jax.ShapeDtypeStruct((192, LANES), F32),
            jax.ShapeDtypeStruct((8, LANES), F32),
        ],
        in_specs=[anywhere] * 7 + [vmem] * 2,
        out_specs=[anywhere] * 4 + [vmem] * 4,
        scratch_shapes=[
            pltpu.VMEM((4,) + rows, BF16),
            pltpu.VMEM((2, 2, 4, 2, PLACES, LANES), BF16),
            pltpu.VMEM((8, LANES, LANES), BF16),
            pltpu.VMEM((8,) + rows, BF16),
            pltpu.VMEM(rows, F32),
            pltpu.VMEM(rows, BF16),
            pltpu.VMEM(rows, F32),
            pltpu.VMEM(rows, BF16),
            pltpu.VMEM((12, 256, REFS), BF16),
            pltpu.VMEM((12, 256, 256), BF16),
            pltpu.VMEM((8,) + rows, BF16),
            pltpu.VMEM((2, 2, 16, PLACES, LANES), BF16),
            pltpu.VMEM((2, 2) + rows, BF16),
            pltpu.VMEM(rows, BF16),
            pltpu.VMEM(rows, BF16),
            pltpu.VMEM((3,) + rows, BF16),
            *[
                pltpu.VMEM(lead + (tall, LANES), BF16)
                for tall in (192, 64)
                for lead in ((2, 4, 2), (4, 2), (3, 2), (2,), ())
            ],
            pltpu.VMEM((2, REFS, LANES), F32),
            pltpu.VMEM(rows, BF16),
            pltpu.VMEM((8, LANES), F32),
            pltpu.VMEM((GROUPS, 8, LANES), F32),
            pltpu.SemaphoreType.DMA((22,)),
            pltpu.SemaphoreType.DMA((16,)),
            pltpu.SemaphoreType.DMA((16,)),
            pltpu.SemaphoreType.DMA((4, GROUPS)),
            pltpu.SemaphoreType.DMA((4, GROUPS)),
            pltpu.SemaphoreType.DMA((18,)),
            pltpu.SemaphoreType.DMA((18,)),
            pltpu.SemaphoreType.DMA((26,)),
            pltpu.SemaphoreType.DMA((26,)),
            pltpu.SemaphoreType.DMA((9, GROUPS)),
            pltpu.SemaphoreType.DMA((9, GROUPS)),
        ],
        compiler_params=pltpu.CompilerParams(
            collective_id=0, has_side_effects=True, vmem_limit_bytes=64_000_000
        ),
    )(queries, keys, values, cotangent, ref_keys, ref_values, weight, taps, bias)
    block_out, grad_q, grad_k, grad_v, grad_rk, grad_rv, grad_w, grad_taps = outs
    return block_out, grad_q, grad_k, grad_v, grad_rk, grad_rv, grad_w.T, grad_taps[:3]


def solution(mesh):
    video = P("frame", None, "head")
    return jax.shard_map(
        per_device,
        mesh=mesh,
        in_specs=(
            video, video, video, P("frame", "head"), P("frame", "head"),
            P("head"), P("head"), P(), P("head", None), P(None, "head"), video,
        ),
        out_specs=(
            video, video, video, video, P("frame", "head"), P("frame", "head"), P("head", "frame"), P(None, "head"),
        ),
        check_vma=False,
    )
```

```python
import functools

import jax
import jax.numpy as jnp
from jax import lax
from jax.experimental import pallas as pl
from jax.experimental.pallas import tpu as pltpu
from jax.sharding import PartitionSpec as P

HEAD_DIM = 128
HEADS_HERE = 3
FRAMES = 32
GROUPS = 16
PLACES = 32
LANES = 384
REFS = 512
MESH = pl.DeviceIdType.MESH
F32 = jnp.float32
BF16 = jnp.bfloat16
SCALE = HEAD_DIM ** (-0.5)


def dot(a, b):
    return lax.dot_general(a, b, (((1,), (0,)), ((), ())), preferred_element_type=F32)


def dot_nt(a, b):
    return lax.dot_general(a, b, (((1,), (1,)), ((), ())), preferred_element_type=F32)


def dot_tn(a, b):
    return lax.dot_general(a, b, (((0,), (0,)), ((), ())), preferred_element_type=F32)


def softmax_rows(scores):
    top = jnp.max(scores, axis=-1, keepdims=True)
    raised = jnp.exp(scores - top)
    return raised / jnp.sum(raised, axis=-1, keepdims=True)


def kernel(
    q_h, k_h, v_h, c_h, rk_h, rv_h, w_h, taps, bias,
    bo_o, dq_o, dk_o, dv_o, drk_o, drv_o, gwt_o, gt_o,
    pos, ref, w3, wide, att, ab, ga, gb, pr, pt, pm, rh, rb, rz, sz,
    dsend, gws, g1, g2, g3, g4, grs, r1, r2, r3, r4, drf, bos, gts, gtr,
    loc_sem, hop_s, hop_r, in_s, in_r, ag_s, ag_r, rs_s, rs_r, out_s, out_r,
):
    f = lax.axis_index("frame")
    h = lax.axis_index("head")
    plane, x = h // 4, h % 4
    near = plane * 4
    away = (1 - plane) * 4
    xr, xl, xo = (x + 1) % 4, (x + 3) % 4, (x + 2) % 4
    right, left, across = near + xr, near + xl, near + xo
    twin, twin_right, twin_left, twin_across = away + x, away + xr, away + xl, away + xo
    zh, y, c = f // 8, (f // 2) % 4, f % 2
    half = FRAMES // 2
    later, sooner = pl.ds(half, half), pl.ds(0, half)
    sides = [pl.ds(0, 16), pl.ds(16, 16)]

    barrier = pltpu.get_barrier_semaphore()

    @pl.loop(1, GROUPS)
    def _(i):
        pl.semaphore_signal(barrier, inc=1, device_id=((f + i) % GROUPS, h), device_id_type=MESH)

    for other in (right, left, twin):
        pl.semaphore_signal(barrier, inc=1, device_id=(f, other), device_id_type=MESH)
    pl.semaphore_wait(barrier, GROUPS + 2)

    def place_in(t, source, i, d, home):
        return pltpu.make_async_remote_copy(
            src_ref=source.at[:, pl.ds(d * PLACES, PLACES), :],
            dst_ref=pos.at[t, pl.ds(home * 2, 2)],
            send_sem=in_s.at[t, i],
            recv_sem=in_r.at[t, i],
            device_id=(d, h),
            device_id_type=MESH,
        )

    def rows_out(t, b, buffer, out, i, d, home):
        return pltpu.make_async_remote_copy(
            src_ref=buffer.at[pl.ds(d * 2, 2), sides[b]],
            dst_ref=out.at[:, pl.ds(home * PLACES + b * 16, 16), :],
            send_sem=out_s.at[t * 2 + b, i],
            recv_sem=out_r.at[t * 2 + b, i],
            device_id=(d, h),
            device_id_type=MESH,
        )

    def own_rows(t, b, buffer, out):
        return pltpu.make_async_copy(
            buffer.at[pl.ds(f * 2, 2), sides[b]],
            out.at[:, pl.ds(f * PLACES + b * 16, 16), :],
            loc_sem.at[14 + t * 2 + b],
        )

    def device(zh_to, y_to, c_to):
        return ((zh_to * 4 + y_to) * 2 + c_to, h)

    z_mate, c_mate = device(1 - zh, y, c), device(zh, y, 1 - c)

    def hop(n, source, target, to):
        return pltpu.make_async_remote_copy(
            src_ref=source, dst_ref=target, send_sem=hop_s.at[n], recv_sem=hop_r.at[n],
            device_id=to, device_id_type=MESH,
        )

    ref_z = [hop(t, s, ref.at[t, zh, y, c], z_mate) for t, s in enumerate((rk_h, rv_h))]
    ref_z_here = [hop(t, s, ref.at[t, 1 - zh, y, c], z_mate) for t, s in enumerate((rk_h, rv_h))]

    def ref_y(n, y_from):
        part = ref.at[:, :, y_from, c]
        return hop(1 + n, part, part, device(zh, (y + n) % 4, c))

    def ref_c(c_from):
        part = ref.at[:, :, :, c_from]
        return hop(5, part, part, c_mate)

    class Sum:
        def __init__(self, base, src, b1, b2, b3, b4):
            self.base, self.src, self.b1, self.b2, self.b3, self.b4 = base, src, b1, b2, b3, b4
            self.to_core = hop(base, src.at[1 - c], b1, c_mate)
            self.to_z = hop(base + 4, b3.at[1 - zh], b4, z_mate)

        def to_y(self, n, y_of):
            return hop(self.base + n, self.src.at[c, y_of], self.b2.at[n - 1], device(zh, (y + n) % 4, c))

        def cores_done(self):
            self.to_core.wait_recv()
            for n in range(4):
                for m in range(2):
                    total = self.src[c, n, m].astype(F32) + self.b1[n, m].astype(F32)
                    self.src[c, n, m] = total.astype(BF16)
            for n in (1, 2, 3):
                self.to_y(n, (y + n) % 4).start()

        def rows_done(self):
            for n in (1, 2, 3):
                self.to_y(n, y).wait_recv()
            for m in range(2):
                total = self.src[c, y, m].astype(F32)
                for n in range(3):
                    total = total + self.b2[n, m].astype(F32)
                self.b3[m] = total.astype(BF16)
            self.to_z.start()

        def total(self):
            self.to_z.wait_recv()
            return self.b3[zh].astype(F32) + self.b4[...].astype(F32)

        def started(self):
            return [self.to_core, self.to_z] + [self.to_y(n, (y + n) % 4) for n in (1, 2, 3)]

    weight_grad = Sum(6, gws, g1, g2, g3, g4)
    ref_grad = Sum(11, grs, r1, r2, r3, r4)

    def taps_out(i, d, home):
        return pltpu.make_async_remote_copy(
            src_ref=gts, dst_ref=gtr.at[home], send_sem=out_s.at[8, i], recv_sem=out_r.at[8, i],
            device_id=(d, h), device_id_type=MESH,
        )

    def start_all(*makers):
        @pl.loop(1, GROUPS)
        def _(i):
            for maker in makers:
                maker(i, (f + i) % GROUPS, f).start()

    def recv_all(*makers):
        @pl.loop(1, GROUPS)
        def _(i):
            for maker in makers:
                maker(i, f, (f + GROUPS - i) % GROUPS).wait_recv()

    def sent_all(*makers):
        @pl.loop(1, GROUPS)
        def _(i):
            for maker in makers:
                maker(i, (f + i) % GROUPS, f).wait_send()

    def gather(b, n, slot, frames, to):
        part = wide.at[slot, frames, sides[b]]
        return pltpu.make_async_remote_copy(
            src_ref=part, dst_ref=part, send_sem=ag_s.at[b * 9 + n], recv_sem=ag_r.at[b * 9 + n],
            device_id=(f, to), device_id_type=MESH,
        )

    whole = pl.ds(0, FRAMES)
    sends = [
        [
            gather(b, 0, h, whole, right),
            gather(b, 1, h, whole, left),
            gather(b, 2, h, whole, twin),
            gather(b, 3, left, sooner, right),
            gather(b, 4, right, later, left),
            gather(b, 5, twin, whole, right),
            gather(b, 6, twin, whole, left),
            gather(b, 7, twin_left, sooner, right),
            gather(b, 8, twin_right, later, left),
        ]
        for b in range(2)
    ]
    arrivals = [
        [
            gather(b, 0, left, whole, right),
            gather(b, 1, right, whole, left),
            gather(b, 2, twin, whole, twin),
            gather(b, 3, across, sooner, right),
            gather(b, 4, across, later, left),
            gather(b, 5, twin_left, whole, right),
            gather(b, 6, twin_right, whole, left),
            gather(b, 7, twin_across, sooner, right),
            gather(b, 8, twin_across, later, left),
        ]
        for b in range(2)
    ]

    def send(b, *which):
        for n in which:
            sends[b][n].start()

    def got(b, *which):
        for n in which:
            arrivals[b][n].wait_recv()

    def scatter(b, o, n, slot, frames, target, to):
        at = (b * 2 + o) * 6 + n
        return pltpu.make_async_remote_copy(
            src_ref=pm.at[slot, frames, sides[b]], dst_ref=target, send_sem=rs_s.at[at], recv_sem=rs_r.at[at],
            device_id=(f, to), device_id_type=MESH,
        )

    ways = [(twin_right, twin_left, twin_across), (right, left, across)]

    def rounds(b, o):
        to_right, to_left, to_across = ways[o]
        return [
            scatter(b, o, 0, to_across, sooner, rh.at[0, o, :, sides[b]], right),
            scatter(b, o, 1, to_across, later, rh.at[1, o, :, sides[b]], left),
            scatter(b, o, 2, to_right, later, rb.at[0, o, later, sides[b]], right),
            scatter(b, o, 3, to_left, sooner, rb.at[1, o, sooner, sides[b]], left),
            scatter(b, o, 4, to_right, sooner, rb.at[0, o, sooner, sides[b]], right),
            scatter(b, o, 5, to_left, later, rb.at[1, o, later, sides[b]], left),
        ]

    turns = [[rounds(b, o) for o in range(2)] for b in range(2)]
    twin_sum = [
        pltpu.make_async_remote_copy(
            src_ref=sz.at[:, sides[b]], dst_ref=rz.at[:, sides[b]], send_sem=rs_s.at[24 + b],
            recv_sem=rs_r.at[24 + b], device_id=(f, twin), device_id_type=MESH,
        )
        for b in range(2)
    ]

    ins = [functools.partial(place_in, t, s) for t, s in enumerate((c_h, q_h, k_h, v_h))]
    own_in = [
        pltpu.make_async_copy(s.at[:, pl.ds(f * PLACES, PLACES), :], pos.at[t, pl.ds(f * 2, 2)], loc_sem.at[t])
        for t, s in enumerate((c_h, q_h, k_h, v_h))
    ]
    own_ref = [
        pltpu.make_async_copy(s, ref.at[t, zh, y, c], loc_sem.at[4 + t]) for t, s in enumerate((rk_h, rv_h))
    ]
    w_in = [
        pltpu.make_async_copy(w_h.at[:, pl.ds(n * LANES, LANES)], w3.at[n], loc_sem.at[6 + n]) for n in range(8)
    ]
    for copy in ref_z + own_ref + own_in[:2]:
        copy.start()
    start_all(ins[0])
    start_all(ins[1])
    start_all(ins[2])
    for copy in own_in[2:] + w_in:
        copy.start()
    drf[...] = jnp.zeros_like(drf)
    gts[...] = jnp.zeros_like(gts)

    own_in[0].wait()
    recv_all(ins[0])
    tap = [taps[n : n + 1, :] for n in range(3)]

    def ct(n):
        return pos[0, n].astype(F32)

    @pl.loop(0, FRAMES - 2)
    def _(n):
        wide[h, n] = (tap[0] * ct(n) + tap[1] * ct(n + 1) + tap[2] * ct(n + 2)).astype(BF16)

    wide[h, FRAMES - 2] = (tap[0] * ct(FRAMES - 2) + tap[1] * ct(FRAMES - 1)).astype(BF16)
    wide[h, FRAMES - 1] = (tap[0] * ct(FRAMES - 1)).astype(BF16)
    send(0, 0, 1, 2)
    for copy in own_ref:
        copy.wait()
    for copy in ref_z_here:
        copy.wait_recv()
    for n in (1, 2, 3):
        ref_y(n, y).start()
    got(0, 0, 1)
    send(0, 3, 4)
    send(1, 0, 1)

    for n in (1, 2, 3):
        ref_y(n, (y + 4 - n) % 4).wait_recv()
    ref_c(c).start()
    own_in[1].wait()
    recv_all(ins[1])
    ref_c(1 - c).wait_recv()

    def head_lanes(a):
        return pl.ds(pl.multiple_of(a * HEAD_DIM, HEAD_DIM), HEAD_DIM)

    def ref_rows(t, lanes):
        return ref[t, :, :, :, :, lanes].reshape(REFS, HEAD_DIM)

    def ref_fwd(b):
        @pl.loop(0, 6)
        def _(n):
            lanes = head_lanes(n // 2)
            frames = pl.ds((n % 2) * half, half)
            query = pos[1, frames, sides[b], lanes].reshape(256, HEAD_DIM)
            weights = softmax_rows(dot_nt(query, ref_rows(0, lanes)) * SCALE).astype(BF16)
            pr[b * 6 + n] = weights
            att[frames, sides[b], lanes] = dot(weights, ref_rows(1, lanes)).reshape(half, 16, HEAD_DIM)

    ref_fwd(0)
    got(0, 2)
    send(0, 5, 6)
    send(1, 2)
    start_all(ins[3])
    ref_fwd(1)
    got(1, 0, 1)
    send(1, 3, 4)

    for copy in w_in:
        copy.wait()

    def rows(array, b, n):
        return array[pl.ds(n * half, half), sides[b]].reshape(256, LANES)

    def add_terms(b, slot, first=False):
        for n in range(2):
            frames = pl.ds(n * half, half)
            terms = dot_nt(rows(wide.at[slot], b, n), w3[slot]).reshape(half, 16, LANES)
            ga[frames, sides[b]] = terms if first else ga[frames, sides[b]] + terms

    add_terms(0, h, True)
    add_terms(0, left)
    add_terms(0, right)
    add_terms(0, twin)
    got(0, 5, 6)
    send(0, 7, 8)
    got(0, 3, 4)
    add_terms(0, across)
    add_terms(0, twin_left)
    add_terms(0, twin_right)
    got(1, 2)
    send(1, 5, 6)
    for t in (2, 3):
        own_in[t].wait()
        recv_all(ins[t])

    def halves(block):
        block = block.astype(F32)
        return [block[:, 8 * n : 8 * n + 8, :].reshape(256, HEAD_DIM).astype(BF16) for n in range(2)]

    def joined(parts):
        return jnp.concatenate([p.reshape(FRAMES, 8, HEAD_DIM) for p in parts], axis=1)

    def time_fwd(b):
        @pl.loop(0, 3)
        def _(a):
            lanes = head_lanes(a)
            queries = halves(pos[1, :, sides[b], lanes])
            keys = halves(pos[2, :, sides[b], lanes])
            values = halves(pos[3, :, sides[b], lanes])
            parts = []
            for m in range(2):
                weights = softmax_rows(dot_nt(queries[m], keys[m]) * SCALE + bias[a]).astype(BF16)
                pt[(b * 3 + a) * 2 + m] = weights
                parts.append(dot(weights, values[m]))
            ab[:, sides[b], lanes] = (att[:, sides[b], lanes] + joined(parts)).astype(BF16)

    def project(b):
        @pl.loop(0, 16)
        def _(n):
            slot, part = n // 2, n % 2
            terms = dot(rows(ab, b, part), w3[slot])
            pm[slot, pl.ds(part * half, half), sides[b]] = terms.astype(BF16).reshape(half, 16, LANES)

    def scatter_first(b):
        for o in range(2):
            for n in range(4):
                turns[b][o][n].start()

    def combine(b, o):
        to_right, to_left, _ = ways[o]

        def add(slot, low, side):
            @pl.loop(0, 2)
            def _(n):
                frames = pl.ds(low + n * 8, 8)
                total = pm[slot, frames, sides[b]].astype(F32) + rh[side, o, pl.ds(n * 8, 8), sides[b]].astype(F32)
                pm[slot, frames, sides[b]] = total.astype(BF16)

        turns[b][o][0].wait_recv()
        add(to_right, 0, 0)
        turns[b][o][4].start()
        turns[b][o][1].wait_recv()
        add(to_left, half, 1)
        turns[b][o][5].start()

    def ref_back(b):
        @pl.loop(0, 6)
        def _(n):
            lanes = head_lanes(n // 2)
            frames = pl.ds((n % 2) * half, half)
            grad = gb[frames, sides[b], lanes].reshape(256, HEAD_DIM)
            query = pos[1, frames, sides[b], lanes].reshape(256, HEAD_DIM)
            weights = pr[b * 6 + n]
            slopes = dot_nt(grad, ref_rows(1, lanes))
            wide_weights = weights.astype(F32)
            level = jnp.sum(wide_weights * slopes, axis=-1, keepdims=True)
            turned = (wide_weights * (slopes - level) * SCALE).astype(BF16)
            att[frames, sides[b], lanes] = dot(turned, ref_rows(0, lanes)).reshape(half, 16, HEAD_DIM)
            drf[0, :, lanes] += dot_tn(turned, query)
            drf[1, :, lanes] += dot_tn(weights, grad)

    def time_back(b):
        @pl.loop(0, 3)
        def _(a):
            lanes = head_lanes(a)
            queries = halves(pos[1, :, sides[b], lanes])
            keys = halves(pos[2, :, sides[b], lanes])
            values = halves(pos[3, :, sides[b], lanes])
            grads = halves(gb[:, sides[b], lanes])
            parts = [[], [], []]
            for m in range(2):
                weights = pt[(b * 3 + a) * 2 + m]
                slopes = dot_nt(grads[m], values[m])
                wide_weights = weights.astype(F32)
                level = jnp.sum(wide_weights * slopes, axis=-1, keepdims=True)
                turned = (wide_weights * (slopes - level) * SCALE).astype(BF16)
                parts[0].append(dot(turned, keys[m]))
                parts[1].append(dot_tn(turned, queries[m]))
                parts[2].append(dot_tn(weights, grads[m]))
            dsend[0, :, sides[b], lanes] = (att[:, sides[b], lanes] + joined(parts[0])).astype(BF16)
            dsend[1, :, sides[b], lanes] = joined(parts[1]).astype(BF16)
            dsend[2, :, sides[b], lanes] = joined(parts[2]).astype(BF16)

    grads_out = [
        [functools.partial(rows_out, t, b, dsend.at[t], o) for t, o in enumerate((dq_o, dk_o, dv_o))] for b in range(2)
    ]
    own_grads = [
        [own_rows(t, b, dsend.at[t], o) for t, o in enumerate((dq_o, dk_o, dv_o))] for b in range(2)
    ]

    def grads_away(b):
        for t in range(3):
            start_all(grads_out[b][t])
        for copy in own_grads[b]:
            copy.start()

    def round_grad(b):
        @pl.loop(0, 4)
        def _(n):
            frames = pl.ds(n * 8, 8)
            gb[frames, sides[b]] = ga[frames, sides[b]].astype(BF16)

    time_fwd(0)
    time_fwd(1)
    project(0)
    scatter_first(0)
    got(0, 7, 8)
    add_terms(0, twin_across)
    round_grad(0)
    ref_back(0)
    got(1, 5, 6)
    send(1, 7, 8)
    time_back(0)
    grads_away(0)
    def plane_sum(b):
        for n in (2, 3, 4, 5):
            turns[b][0][n].wait_recv()

        @pl.loop(0, 4)
        def _(n):
            frames = pl.ds(n * 8, 8)
            total = pm[twin, frames, sides[b]].astype(F32)
            for side in range(2):
                total = total + rb[side, 0, frames, sides[b]].astype(F32)
            sz[frames, sides[b]] = total.astype(BF16)

        twin_sum[b].start()

    combine(0, 0)
    project(1)
    combine(0, 1)
    scatter_first(1)
    add_terms(1, h, True)
    for slot in (left, right, twin):
        add_terms(1, slot)
    got(1, 3, 4)
    for slot in (across, twin_left, twin_right):
        add_terms(1, slot)
    got(1, 7, 8)
    @pl.loop(0, 8)
    def _(slot):
        total = dot_tn(wide[slot].reshape(1024, LANES), ab[...].reshape(1024, LANES)).astype(BF16)
        for j in range(2):
            gws[j, slot % 4, slot // 4] = total[192 * j : 192 * j + 192]

    weight_grad.to_core.start()
    plane_sum(0)
    add_terms(1, twin_across)
    round_grad(1)
    ref_back(1)
    weight_grad.cores_done()
    combine(1, 0)
    time_back(1)
    grads_away(1)
    combine(1, 1)
    for d in range(GROUPS):
        for t in range(2):
            part = drf[t, d * PLACES : (d + 1) * PLACES].astype(BF16)
            grs[d % 2, (d // 2) % 4, d // 8, t * PLACES : (t + 1) * PLACES] = part
    ref_grad.to_core.start()
    plane_sum(1)
    ref_grad.cores_done()

    def plane_own(b):
        for n in (2, 3, 4, 5):
            turns[b][1][n].wait_recv()

    def output(b):
        @pl.loop(0, 4)
        def _(n):
            frames = pl.ds(n * 8, 8)
            total = pm[h, frames, sides[b]].astype(F32) + rz[frames, sides[b]].astype(F32)
            for side in range(2):
                total = total + rb[side, 1, frames, sides[b]].astype(F32)
            ga[frames, sides[b]] = total.astype(BF16).astype(F32)

        def cs(n):
            return pos[0, n, sides[b]].astype(F32)

        def mixed(n):
            return ga[n, sides[b]]

        bos[0, sides[b]] = (tap[0] * mixed(0)).astype(BF16)
        bos[1, sides[b]] = (tap[0] * mixed(1) + tap[1] * mixed(0)).astype(BF16)
        sums = (cs(0) * mixed(0) + cs(1) * mixed(1), cs(1) * mixed(0), jnp.zeros((16, LANES), F32))

        def mix(n, carry):
            now, back, older = mixed(n), mixed(n - 1), mixed(n - 2)
            bos[n, sides[b]] = (tap[0] * now + tap[1] * back + tap[2] * older).astype(BF16)
            cn = cs(n)
            return (carry[0] + cn * now, carry[1] + cn * back, carry[2] + cn * older)

        sums = lax.fori_loop(2, FRAMES, mix, sums)
        start_all(block_out[b])
        own_block[b].start()
        for n in range(3):
            gts[n : n + 1, :] += jnp.sum(sums[n], axis=0, keepdims=True)

    block_out = [functools.partial(rows_out, 3, b, bos, bo_o) for b in range(2)]
    own_block = [own_rows(3, b, bos, bo_o) for b in range(2)]
    plane_own(0)
    twin_sum[0].wait_recv()
    output(0)
    plane_own(1)
    weight_grad.rows_done()
    ref_grad.rows_done()
    twin_sum[1].wait_recv()
    output(1)
    start_all(taps_out)
    gwt_o[...] = weight_grad.total()
    refs = ref_grad.total()
    drk_o[...] = refs[:PLACES]
    drv_o[...] = refs[PLACES:]

    recv_all(taps_out)
    gt_o[...] = lax.fori_loop(1, GROUPS, lambda i, total: total + gtr[(f + i) % GROUPS], gts[...])
    recv_all(*grads_out[0], *grads_out[1])
    recv_all(*block_out)
    for copy in own_grads[0] + own_grads[1] + own_block:
        copy.wait()
    sent_all(*ins, taps_out, *grads_out[0], *grads_out[1], *block_out)
    steps = ref_z + [ref_y(n, y) for n in (1, 2, 3)] + [ref_c(c)]
    steps += weight_grad.started() + ref_grad.started()
    for b in range(2):
        steps += sends[b] + turns[b][0] + turns[b][1] + [twin_sum[b]]
    for copy in steps:
        copy.wait_send()


def per_device(queries, keys, values, ref_keys, ref_values, rate_scale, rate_reach, starts, weight, taps, cotangent):
    places = jnp.arange(256, dtype=jnp.int32)
    frame, place = places // 8, places % 8
    distance = jnp.abs(frame[:, None] - frame[None, :]).astype(F32)
    first = jnp.repeat(starts, 8)
    allowed = (
        (place[:, None] == place[None, :])
        & (frame[None, :] <= frame[:, None])
        & (frame[None, :] >= first[:, None])
    )
    penalty = -rate_scale[:, None, None] * jnp.log1p(rate_reach[:, None, None] * distance[None])
    bias = jnp.where(allowed[None], penalty, -1e30)

    anywhere = pl.BlockSpec(memory_space=pl.ANY)
    vmem = pl.BlockSpec(memory_space=pltpu.VMEM)
    rows = (FRAMES, PLACES, LANES)
    video = jax.ShapeDtypeStruct(queries.shape, BF16)
    refs = jax.ShapeDtypeStruct(ref_keys.shape, F32)
    outs = pl.pallas_call(
        kernel,
        out_shape=[
            video, video, video, video, refs, refs,
            jax.ShapeDtypeStruct((192, LANES), F32),
            jax.ShapeDtypeStruct((8, LANES), F32),
        ],
        in_specs=[anywhere] * 7 + [vmem] * 2,
        out_specs=[anywhere] * 4 + [vmem] * 4,
        scratch_shapes=[
            pltpu.VMEM((4,) + rows, BF16),
            pltpu.VMEM((2, 2, 4, 2, PLACES, LANES), BF16),
            pltpu.VMEM((8, LANES, LANES), BF16),
            pltpu.VMEM((8,) + rows, BF16),
            pltpu.VMEM(rows, F32),
            pltpu.VMEM(rows, BF16),
            pltpu.VMEM(rows, F32),
            pltpu.VMEM(rows, BF16),
            pltpu.VMEM((12, 256, REFS), BF16),
            pltpu.VMEM((12, 256, 256), BF16),
            pltpu.VMEM((8,) + rows, BF16),
            pltpu.VMEM((2, 2, 16, PLACES, LANES), BF16),
            pltpu.VMEM((2, 2) + rows, BF16),
            pltpu.VMEM(rows, BF16),
            pltpu.VMEM(rows, BF16),
            pltpu.VMEM((3,) + rows, BF16),
            *[
                pltpu.VMEM(lead + (tall, LANES), BF16)
                for tall in (192, 64)
                for lead in ((2, 4, 2), (4, 2), (3, 2), (2,), ())
            ],
            pltpu.VMEM((2, REFS, LANES), F32),
            pltpu.VMEM(rows, BF16),
            pltpu.VMEM((8, LANES), F32),
            pltpu.VMEM((GROUPS, 8, LANES), F32),
            pltpu.SemaphoreType.DMA((22,)),
            pltpu.SemaphoreType.DMA((16,)),
            pltpu.SemaphoreType.DMA((16,)),
            pltpu.SemaphoreType.DMA((4, GROUPS)),
            pltpu.SemaphoreType.DMA((4, GROUPS)),
            pltpu.SemaphoreType.DMA((18,)),
            pltpu.SemaphoreType.DMA((18,)),
            pltpu.SemaphoreType.DMA((26,)),
            pltpu.SemaphoreType.DMA((26,)),
            pltpu.SemaphoreType.DMA((9, GROUPS)),
            pltpu.SemaphoreType.DMA((9, GROUPS)),
        ],
        compiler_params=pltpu.CompilerParams(
            collective_id=0, has_side_effects=True, vmem_limit_bytes=64_000_000
        ),
    )(queries, keys, values, cotangent, ref_keys, ref_values, weight, taps, bias)
    block_out, grad_q, grad_k, grad_v, grad_rk, grad_rv, grad_w, grad_taps = outs
    return block_out, grad_q, grad_k, grad_v, grad_rk, grad_rv, grad_w.T, grad_taps[:3]


def solution(mesh):
    video = P("frame", None, "head")
    return jax.shard_map(
        per_device,
        mesh=mesh,
        in_specs=(
            video, video, video, P("frame", "head"), P("frame", "head"),
            P("head"), P("head"), P(), P("head", None), P(None, "head"), video,
        ),
        out_specs=(
            video, video, video, video, P("frame", "head"), P("frame", "head"), P("head", "frame"), P(None, "head"),
        ),
        check_vma=False,
    )
```
